32 devices in a mesh: tgt: 4 (over y, x), qry: 8 (over z, core).
Axes of the slice: x: 2, y: 2, z: 4, core: 2. Of those that a mesh axis runs over, the one named last changes fastest.
Arguments:
- query_feats: bfloat16 [4096, 256], P('qry'), may hold values from -6 to 6
- target_feats: bfloat16 [160, 128, 256], P('tgt', 'qry'), may hold values from -6 to 6
- conv_weight: bfloat16 [64, 64], replicated, may hold values from -0.75 to 0.75
- conv_bias: float32 [64], replicated, may hold values from -4 to 4
- key_weight: bfloat16 [64, 128], replicated, may hold values from -0.75 to 0.75
- value_weight: bfloat16 [64, 128], replicated, may hold values from -2 to 2
- latents: bfloat16 [8, 128], replicated, may hold values from -5 to 5
- query_weight: bfloat16 [128, 128], replicated, may hold values from -0.5 to 0.5
- memkey_weight: bfloat16 [128, 128], replicated, may hold values from -0.5 to 0.5
- memvalue_weight: bfloat16 [128, 128], replicated, may hold values from -0.5 to 0.5
Outputs:
- cost_memory: bfloat16 [8, 4096, 128], P('tgt', 'qry')
The draws below stay inside these ranges and needn't reach their ends.
All inputs are finite; a program needn't handle non-finite values.
Results may differ from the reference program's by a relative error of at most 0.0068.
Values may be sent and summed in bfloat16 or wider, within the bound.
No kernel may reach another device: no remote copies, remote signals or barrier semaphores. Data moves between devices by JAX's collectives and lax.ppermute only.
A program may use at most 192 MiB of HBM per device.

```python
import math
import jax
import jax.numpy as jnp
from jax import lax

C = 256
DP = 64
DL = 128
K = 8
PATCH = 8
QDEV = 512
TH = 160
TW = 128
NQ = 4096


def block_levels(rng, shape, pieces, low, largest):
    def one(dim, parts):
        draws = jax.random.uniform(jax.random.fold_in(jax.random.fold_in(rng, 6), dim), (parts,), jnp.float32, low / len(pieces), largest / len(pieces))
        return jnp.repeat(jnp.exp(draws), shape[dim] // parts).reshape((-1,) + (1,) * (len(shape) - dim - 1))

    factor_of = one(*pieces[0])
    for cut in pieces[1:]:
        factor_of = factor_of * one(*cut)
    return factor_of


def bell_draw(stream_key, extent, deviation, reach, split=(), dtype=jnp.bfloat16):
    loudness = block_levels(stream_key, extent, split, -0.22, 0.18) if split else 1.0
    drawn = jax.random.normal(stream_key, extent, jnp.float32) * deviation * loudness
    return jnp.minimum(jnp.maximum(drawn, -reach), reach).astype(dtype)


def setup_inputs(seed: int = 0) -> dict:
    splits = jax.random.split(jax.random.key(seed), 11)
    query_feats = bell_draw(splits[0], (NQ, C), 1.0, 6.0, ((0, 8),))
    target_feats = bell_draw(splits[1], (TH, TW, C), 1.0, 6.0, ((0, 4), (1, 8)))
    conv_weight = bell_draw(splits[2], (PATCH * PATCH, DP), (PATCH * PATCH) ** -0.5, 0.75)
    conv_bias = bell_draw(splits[3], (DP,), 0.7, 4.0, (), jnp.float32)
    key_weight = bell_draw(splits[4], (DP, DL), DP ** -0.5, 0.75)
    value_weight = bell_draw(splits[5], (DP, DL), (DP // 8) ** -0.5, 2.0)
    latents = bell_draw(splits[6], (K, DL), 1.0, 5.0)
    query_weight = bell_draw(splits[7], (DL, DL), DL ** -0.5, 0.5)
    memkey_weight = bell_draw(splits[8], (DL, DL), DL ** -0.5, 0.5)
    memvalue_weight = bell_draw(splits[9], (DL, DL), DL ** -0.5, 0.5)
    return {"query_feats": query_feats, "target_feats": target_feats, "conv_weight": conv_weight, "conv_bias": conv_bias, "key_weight": key_weight, "value_weight": value_weight, "latents": latents, "query_weight": query_weight, "memkey_weight": memkey_weight, "memvalue_weight": memvalue_weight}


score_gain = 4.0
memory_gain = 3.0

def rms_norm(values):
    return values * lax.rsqrt(lax.optimization_barrier(jnp.mean(values * values, axis=-1, keepdims=True)) + 1e-05)

def reference(query_feats, target_feats, conv_weight, conv_bias, key_weight, value_weight, latents, query_weight, memkey_weight, memvalue_weight):
    channels = query_feats.shape[1]
    flat_targets = target_feats.reshape(-1, channels)
    probe = (jnp.dot(key_weight, latents.T, preferred_element_type=jnp.float32) * (score_gain / math.sqrt(DL))).astype(jnp.bfloat16)
    probe_wide = probe.astype(jnp.float32)
    value_wide = value_weight.astype(jnp.float32)

    def encode(query_block):
        block_rows = query_block.shape[0]
        cost_tile = (jnp.dot(query_block, flat_targets.T, preferred_element_type=jnp.float32) / math.sqrt(channels)).astype(jnp.bfloat16)
        tiles = cost_tile.reshape(block_rows, TH // PATCH, PATCH, TW // PATCH, PATCH).transpose(0, 1, 3, 2, 4).reshape(-1, PATCH * PATCH)
        embedded = jnp.dot(tiles, conv_weight, preferred_element_type=jnp.float32) + conv_bias
        normed = rms_norm(embedded).astype(jnp.bfloat16).reshape(block_rows, -1, DP)
        normed_wide = normed.astype(jnp.float32)
        weights = jnp.exp(jnp.einsum('qpd,dk->qpk', normed_wide, probe_wide))
        totals = lax.optimization_barrier(jnp.sum(weights, axis=1))
        pooled = jnp.einsum('qpk,qpd->qkd', weights.astype(jnp.bfloat16).astype(jnp.float32), normed_wide)
        attended = (pooled / totals[:, :, None]).astype(jnp.bfloat16)
        return jnp.einsum('qkd,de->kqe', attended.astype(jnp.float32), value_wide).astype(jnp.bfloat16)
    query_blocks = query_feats.reshape(NQ // QDEV, QDEV, channels)
    memory = lax.map(encode, query_blocks)
    memory = memory.transpose(1, 0, 2, 3).reshape(K, NQ, DL)
    memory_wide = memory.astype(jnp.float32)
    mem_queries = rms_norm(jnp.einsum('kqd,de->kqe', memory_wide, query_weight.astype(jnp.float32))).astype(jnp.bfloat16)
    mem_keys = rms_norm(jnp.einsum('kqd,de->kqe', memory_wide, memkey_weight.astype(jnp.float32))).astype(jnp.bfloat16)
    mem_values = jnp.einsum('kqd,de->kqe', memory_wide, memvalue_weight.astype(jnp.float32)).astype(jnp.bfloat16)
    scale = memory_gain / math.sqrt(DL)

    def attend(inputs):
        query_block, memory_block = inputs
        scores = jnp.einsum('kqd,knd->kqn', query_block.astype(jnp.float32), mem_keys.astype(jnp.float32)) * scale
        weights = jnp.exp(scores)
        totals = lax.optimization_barrier(jnp.sum(weights, axis=-1))
        mixed = jnp.einsum('kqn,knd->kqd', weights.astype(jnp.bfloat16).astype(jnp.float32), mem_values.astype(jnp.float32))
        return (memory_block.astype(jnp.float32) + mixed / totals[:, :, None]).astype(jnp.bfloat16)
    query_split = mem_queries.reshape(K, NQ // QDEV, QDEV, DL).transpose(1, 0, 2, 3)
    memory_split = memory.reshape(K, NQ // QDEV, QDEV, DL).transpose(1, 0, 2, 3)
    result = lax.map(attend, (query_split, memory_split))
    return result.transpose(1, 0, 2, 3).reshape(K, NQ, DL)
```

```python
import functools
import math

import jax
import jax.numpy as jnp
from jax import lax
from jax.experimental import pallas as pl
from jax.experimental.pallas import tpu as pltpu
from jax.sharding import PartitionSpec as P

PATCH = 8
LANES = 128
EPS = 1e-05
score_gain = 4.0
memory_gain = 3.0
F32 = jnp.float32
BF16 = jnp.bfloat16


def vmem(count):
    return [pl.BlockSpec(memory_space=pltpu.VMEM)] * count


def nt_dot(a, b):
    return lax.dot_general(a, b, (((1,), (1,)), ((), ())), preferred_element_type=F32)


def pool_kernel(dims, first, last, *refs):
    embed, latent, groups, slot_share = dims
    refs = list(refs)
    group_ref = refs.pop(0) if last else None
    one_ref, two_ref, fold_ref, query_ref, bias_ref, score_bias_ref = refs[:6]
    refs = refs[6:]
    if not first:
        pooled_in, totals_in, scaled_in = refs[:3]
        refs = refs[3:]
    if last:
        outs, refs = refs[: groups + 1], refs[groups + 1 :]
        pooled_out, totals_out, scaled_out, folded, costs, weights = refs
    else:
        pooled_out, totals_out, scaled_out, folded, costs, weights = refs
    rows, cols, channels = one_ref.shape
    queries = query_ref.shape[0]
    span = embed + latent
    bands = rows // PATCH
    band_rows = fold_ref.shape[0]
    patches = 2 * bands * (cols // PATCH)

    for index, block in enumerate((one_ref, two_ref)):
        for band in range(bands):
            pixels = block[band * PATCH : (band + 1) * PATCH].reshape(PATCH * cols, channels)
            made = jnp.dot(fold_ref[...], pixels, preferred_element_type=F32)
            start = (index * bands + band) * band_rows
            folded[start : start + band_rows, :] = made.astype(BF16)

    query = query_ref[...]
    for index in range(bands):
        start = index * 2 * band_rows
        costs[start : start + 2 * band_rows, :] = nt_dot(folded[start : start + 2 * band_rows, :], query)

    bias = jnp.broadcast_to(bias_ref[:, :1], (embed, queries))
    score_bias = jnp.broadcast_to(score_bias_ref[:, :1], (latent, queries))

    def weigh(patch, carry):
        totals, scaled = carry
        start = pl.multiple_of(patch * span, 8)
        embedded = costs[pl.ds(start, embed), :] + bias
        mean = jnp.sum(embedded * embedded, axis=0, keepdims=True) * (1.0 / embed)
        factor = lax.rsqrt(mean + EPS)
        raw = costs[pl.ds(pl.multiple_of(start + embed, 8), latent), :] + score_bias
        weight = jnp.exp(raw * factor)
        product = weight * factor
        weights[patch] = product
        return totals + weight, scaled + product

    zero = jnp.zeros((latent, queries), F32)
    carry = (zero, zero) if first else (totals_in[...], scaled_in[...])
    totals, scaled = lax.fori_loop(0, patches, weigh, carry, unroll=2)
    totals_out[...] = totals
    scaled_out[...] = scaled

    depth = 32
    for lane in range(queries // LANES):
        at = slice(lane * LANES, (lane + 1) * LANES)
        for part in range(embed // depth):
            below = slice(part * depth, (part + 1) * depth)

            def gather(patch, sums):
                start = pl.multiple_of(patch * span + part * depth, 8)
                values = costs[pl.ds(start, depth), at]
                return tuple(
                    sums[k] + weights[patch, pl.ds(k, 1), at] * values for k in range(latent)
                )

            if first:
                begin = tuple(jnp.zeros((depth, LANES), F32) for _ in range(latent))
            else:
                begin = tuple(pooled_in[k, below, at] for k in range(latent))
            sums = lax.fori_loop(0, patches, gather, begin, unroll=4)
            for k in range(latent):
                pooled_out[k, below, at] = sums[k]

    if last:
        group = group_ref[0]
        bias = jnp.broadcast_to(bias_ref[:, :1], (embed, queries))
        width = slot_share * embed
        for step in range(groups):
            slot = (group ^ step) * slot_share
            sums, counts = [], []
            for j in range(slot_share):
                scale = scaled_out[pl.ds(slot + j, 1), :]
                sums.append(pooled_out[slot + j] + bias * scale)
                counts.append(totals_out[pl.ds(slot + j, 1), :])
            if step == 0:
                for j in range(slot_share):
                    outs[0][j * embed : (j + 1) * embed, :] = sums[j]
                    outs[1][j : j + 1, :] = counts[j]
            else:
                out = outs[step + 1]
                for j in range(slot_share):
                    out[j * embed : (j + 1) * embed, :] = sums[j].astype(BF16)
                high = [c.astype(BF16).astype(F32) for c in counts]
                low = [c - h for c, h in zip(counts, high)]
                tail = jnp.concatenate(
                    high + low + [jnp.zeros((16 - 2 * slot_share, queries), F32)], axis=0
                )
                out[width : width + 16, :] = tail.astype(BF16)


def pool_pair(pair, fold, query, bias, score_bias, state, group, dims):
    embed, latent, groups, slot_share = dims
    first, last = state is None, group is not None
    one, two = pair
    rows, cols, channels = one.shape
    queries = query.shape[0]
    patches = 2 * (rows // PATCH) * (cols // PATCH)
    height = patches * (embed + latent)
    sums = [
        ((latent, embed, queries), F32),
        ((latent, queries), F32),
        ((latent, queries), F32),
    ]
    scratch = [
        pltpu.VMEM((height, channels), BF16),
        pltpu.VMEM((height, queries), F32),
        pltpu.VMEM((patches, latent, queries), F32),
    ]
    operands = [one, two, fold, query, bias, score_bias]
    specs = vmem(len(operands))
    if not first:
        operands += list(state)
        specs += vmem(3)
    if last:
        operands = [group] + operands
        specs = [pl.BlockSpec(memory_space=pltpu.SMEM)] + specs
        width = slot_share * embed
        outs = [((width, queries), F32), ((slot_share, queries), F32)]
        outs += [((width + 16, queries), BF16)] * (groups - 1)
        scratch = [pltpu.VMEM(*s) for s in sums] + scratch
    else:
        outs = sums
    flops = 2 * height * channels * (queries + 2 * PATCH * PATCH) + 16 * height * queries
    return pl.pallas_call(
        functools.partial(pool_kernel, dims, first, last),
        out_shape=[jax.ShapeDtypeStruct(*o) for o in outs],
        in_specs=specs,
        out_specs=vmem(len(outs)),
        scratch_shapes=scratch,
        cost_estimate=pl.CostEstimate(
            flops=flops, bytes_accessed=4 << 20, transcendentals=patches * latent * queries
        ),
        name="pool_last" if last else "pool_first" if first else "pool_next",
    )(*operands)


def combine_kernel(embed, slot_share, own_ref, counts_ref, *refs):
    arrived, out_ref = refs[:-1], refs[-1]
    width = slot_share * embed
    pooled = own_ref[...]
    totals = counts_ref[...]
    for ref in arrived:
        pooled = pooled + ref[:width, :].astype(F32)
        tail = ref[width : width + 16, :].astype(F32)
        totals = totals + tail[:slot_share] + tail[slot_share : 2 * slot_share]
    parts = [
        pooled[j * embed : (j + 1) * embed] / totals[j : j + 1] for j in range(slot_share)
    ]
    out_ref[...] = jnp.concatenate(parts, axis=0).T.astype(BF16)


def combine(own, counts, arrived, embed, slot_share):
    width, queries = own.shape
    return pl.pallas_call(
        functools.partial(combine_kernel, embed, slot_share),
        out_shape=jax.ShapeDtypeStruct((queries, width), BF16),
        in_specs=vmem(2 + len(arrived)),
        out_specs=pl.BlockSpec(memory_space=pltpu.VMEM),
        cost_estimate=pl.CostEstimate(
            flops=8 * width * queries, bytes_accessed=1 << 20, transcendentals=0
        ),
        name="combine",
    )(own, counts, *arrived)


def unit_rows(values):
    return values * lax.rsqrt(jnp.mean(values * values, axis=-1, keepdims=True) + EPS)


def mix_kernel(dims, first, last, *refs):
    embed, slot_share, scale = dims
    refs = list(refs)
    one_ref, two_ref, wide_ref, key_ref = refs[:4]
    refs = refs[4:]
    if first:
        query_weight = refs.pop(0)
        sums_in = None
    else:
        queries_in = refs.pop(0)
        sums_in = refs.pop(0)
    if last:
        memory_in, final_ref, out_ref = refs[:3]
        refs = refs[3:]
        sums_out = refs.pop(0)
    elif first:
        sums_out, queries_out, memory_out = refs[:3]
        refs = refs[3:]
    else:
        sums_out = refs.pop(0)
    rows = one_ref.shape[0]
    wide = wide_ref.shape[1] // slot_share
    if first:
        memory = jnp.dot(one_ref[...], wide_ref[...], preferred_element_type=F32).astype(BF16)
        for s in range(slot_share):
            part = memory[:, s * wide : (s + 1) * wide]
            memory_out[s] = part
            made = jnp.dot(part, query_weight[...], preferred_element_type=F32)
            queries_out[s] = unit_rows(made).astype(BF16)
        queries_in = queries_out
    tile = 256
    count = queries_in.shape[1]
    for index, block in enumerate((one_ref, two_ref)):
        attended = block[...]
        memory = jnp.dot(attended, wide_ref[...], preferred_element_type=F32).astype(BF16)
        lanes = lax.broadcasted_iota(jnp.int32, attended.shape, 1)
        for s in range(slot_share):
            made = jnp.dot(
                memory[:, s * wide : (s + 1) * wide], key_ref[...], preferred_element_type=F32
            )
            keys = unit_rows(made).astype(BF16)
            if slot_share == 1:
                values = jnp.concatenate([attended, jnp.ones_like(attended)], axis=1)
            else:
                inside = (lanes >= s * embed) & (lanes < (s + 1) * embed)
                values = jnp.where(inside, attended, jnp.ones_like(attended))
            for start in range(0, count, tile):
                at = slice(start, start + tile)
                scores = nt_dot(queries_in[s, at, :], keys)
                weights = jnp.exp2(scores * (scale * math.log2(math.e))).astype(BF16)
                added = jnp.dot(weights, values, preferred_element_type=F32)
                if index == 0 and sums_in is None:
                    sums_out[s, at, :] = added
                elif index == 0:
                    sums_out[s, at, :] = sums_in[s, at, :] + added
                else:
                    sums_out[s, at, :] += added
    if last:
        for s in range(slot_share):
            sums = sums_out[s]
            ratio = sums / pltpu.roll(sums, embed, 1)
            lanes = lax.broadcasted_iota(jnp.int32, sums.shape, 1)
            inside = (lanes >= s * embed) & (lanes < (s + 1) * embed)
            ratio = jnp.where(inside, ratio, 0.0)
            mixed = jnp.dot(
                ratio, final_ref[s], preferred_element_type=F32, precision=lax.Precision.HIGHEST
            )
            out_ref[s] = (memory_in[s].astype(F32) + mixed).astype(BF16)


def mix_pair(pair, wide, key_weight, query_weight, queries, sums, memory, final, dims):
    embed, slot_share, scale = dims
    first, last = queries is None, final is not None
    one, two = pair
    rows = one.shape[0]
    latent_width = key_weight.shape[0]
    block = (slot_share, rows, latent_width)
    sums_type = ((slot_share, rows, 2 * embed), F32)
    operands = [one, two, wide, key_weight]
    scratch = []
    if first:
        operands.append(query_weight)
        outs = [sums_type, (block, BF16), (block, BF16)]
    else:
        operands += [queries, sums]
        outs = [sums_type]
    if last:
        operands += [memory, final]
        outs = [(block, BF16)]
        scratch = [pltpu.VMEM(*sums_type)]
    made = pl.pallas_call(
        functools.partial(mix_kernel, dims, first, last),
        out_shape=[jax.ShapeDtypeStruct(*o) for o in outs],
        in_specs=vmem(len(operands)),
        out_specs=vmem(len(outs)),
        scratch_shapes=scratch,
        cost_estimate=pl.CostEstimate(
            flops=16 * slot_share * rows * rows * latent_width,
            bytes_accessed=2 << 20,
            transcendentals=2 * slot_share * rows * rows,
        ),
        name="mix_last" if last else "mix_first" if first else "mix_next",
    )(*operands)
    return made


def exchange(x, axis):
    size = lax.axis_size(axis)

    def swap(value, step):
        return lax.ppermute(value, axis, [(i, i ^ step) for i in range(size)])

    if size != 8:
        pairs = [(x, swap(x, 1))]
        for step in range(2, size, 2):
            far = swap(x, step)
            pairs.append((far, swap(far, 1)))
        return pairs
    middle = [(i, i ^ 6) for i in (2, 3, 4, 5)]
    relay = [(2, 0), (3, 1), (4, 6), (5, 7)]
    far = swap(x, 4)
    near = swap(x, 2)
    held, far = lax.optimization_barrier((x, far))
    inner = lax.ppermute(held, axis, middle)
    outer = lax.ppermute(far, axis, relay)
    place = lax.axis_index(axis)
    inside = (place >= 2) & (place < 6)
    rest = jnp.where(inside, inner, outer)
    return [(x, swap(x, 1)), (near, swap(near, 1)), (far, swap(far, 1)), (rest, swap(rest, 1))]


def local(
    query_feats,
    target_feats,
    conv_weight,
    conv_bias,
    key_weight,
    value_weight,
    latents,
    query_weight,
    memkey_weight,
    memvalue_weight,
):
    query_rows, channels = query_feats.shape
    latent_count, latent_width = latents.shape
    embed = conv_weight.shape[1]
    cols = target_feats.shape[1]
    groups = lax.axis_size("tgt")
    slot_share = latent_count // groups
    pairs = exchange(target_feats, "qry")

    probe = (
        jnp.dot(key_weight, latents.T, preferred_element_type=F32)
        * (score_gain / math.sqrt(latent_width))
    ).astype(BF16)
    root = 1.0 / math.sqrt(channels)
    scoring = jnp.dot(conv_weight, probe, preferred_element_type=F32)
    joint = jnp.concatenate([conv_weight.astype(F32), scoring], axis=1) * root
    across = cols // PATCH
    kernel = joint.reshape(PATCH, PATCH, embed + latent_count).transpose(2, 0, 1)
    fold = jnp.einsum("ab,fij->afibj", jnp.eye(across, dtype=F32), kernel)
    fold = fold.reshape(across * (embed + latent_count), PATCH * cols).astype(BF16)
    bias = jnp.broadcast_to(conv_bias[:, None], (embed, LANES))
    score_bias = jnp.sum(conv_bias[:, None] * probe.astype(F32), axis=0)
    score_bias = jnp.broadcast_to(score_bias[:, None], (latent_count, LANES))

    dims = (embed, latent_count, groups, slot_share)
    group = lax.axis_index("tgt").astype(jnp.int32).reshape(1)
    state = None
    for index, pair in enumerate(pairs):
        last = index == len(pairs) - 1
        state = pool_pair(
            pair, fold, query_feats, bias, score_bias, state, group if last else None, dims
        )
    own, counts, sends = state[0], state[1], state[2:]
    arrived = [
        lax.ppermute(sends[step - 1], "tgt", [(i, i ^ step) for i in range(groups)])
        for step in range(1, groups)
    ]
    attended = combine(own, counts, arrived, embed, slot_share)

    blocks = exchange(attended, "qry")
    wide = jnp.einsum("ab,de->adbe", jnp.eye(slot_share, dtype=BF16), value_weight)
    wide = wide.reshape(slot_share * embed, slot_share * latent_width)
    through = jnp.dot(
        value_weight.astype(F32), memvalue_weight.astype(F32), precision=lax.Precision.HIGHEST
    )
    final = jnp.einsum("sa,de->sade", jnp.eye(slot_share, 2, dtype=F32), through)
    final = final.reshape(slot_share, 2 * embed, latent_width)
    dims = (embed, slot_share, memory_gain / math.sqrt(latent_width))
    queries = sums = memory = None
    for index, pair in enumerate(blocks):
        last = index == len(blocks) - 1
        made = mix_pair(
            pair, wide, memkey_weight, query_weight, queries, sums, memory, final if last else None, dims
        )
        if index == 0:
            sums, queries, memory = made
        else:
            sums = made[0]
    return sums


def solution(mesh):
    return jax.shard_map(
        local,
        mesh=mesh,
        in_specs=(P("qry", None), P("tgt", "qry", None), P(), P(), P(), P(), P(), P(), P(), P()),
        out_specs=P("tgt", "qry", None),
        check_vma=False,
    )
```
